32 devices in a mesh: freq: 4 (over y, x), panel: 8 (over z, core).
Axes of the slice: x: 2, y: 2, z: 4, core: 2. Of those that a mesh axis runs over, the one named last changes fastest.
Arguments:
- traces: bfloat16 [640, 640, 1024], P('panel', 'freq'), may hold values from -6 to 6
- filters: float32 [16, 7, 64], replicated, may hold values from -0.25 to 0.25
Outputs:
- primaries: bfloat16 [640, 640, 1024], P('panel', 'freq')
The draws below stay inside these ranges and needn't reach their ends.
All inputs are finite; a program needn't handle non-finite values.
Results may differ from the reference program's by a relative error of at most 0.0095.
Values may be sent and summed in bfloat16 or wider, within the bound.
A program may use at most 192 MiB of HBM per device.

```python
import math
from functools import partial
import jax
import jax.numpy as jnp
from jax import lax

NS = 640
NR = 640
NT = 1024
NF = 96
FLO = 8
TAPS = 64
SPAN = 7
RWIN = 40
NWIN = 16


def block_scale(own_key, shape, shards, low, largest):
    factor_of, own = 1.0, jax.random.fold_in(own_key, 6)
    for axis_at, shards_of in shards:
        heights = jnp.exp(jax.random.uniform(jax.random.fold_in(own, axis_at), (shards_of,), jnp.float32, low / len(shards), largest / len(shards)))
        factor_of = factor_of * jnp.repeat(heights, shape[axis_at] // shards_of).reshape([-1 if axis == axis_at else 1 for axis in range(len(shape))])
    return factor_of


def bell_draw(key, shape, spread, most, cuts=(), kind=jnp.bfloat16):
    entries = spread * jax.random.normal(key, shape, jnp.float32)
    if cuts:
        entries = entries * block_scale(key, shape, cuts, -0.22, 0.18)
    return jnp.clip(entries, -most, most).astype(kind)


def setup_inputs(seed: int = 0) -> dict:
    streams_of = jax.random.split(jax.random.key(seed), 3)
    traces = bell_draw(streams_of[0], (NS, NR, NT), 1.0, 6.0, ((0, 8), (1, 4)))
    filters = bell_draw(streams_of[1], (NWIN, SPAN, TAPS), (SPAN * TAPS) ** -0.5, 0.25, (), jnp.float32)
    return {"traces": traces, "filters": filters}


def wave_table(freq_bins, sample_index):
    phases = freq_bins[:, None] * sample_index[None, :] % NT
    angles = phases.astype(jnp.float32) * jnp.float32(2.0 * math.pi / NT)
    return (jnp.cos(angles), jnp.sin(angles))

def complex_product(left_side, right_side):
    factor_product = partial(jnp.einsum, 'gjo,god->gjd', precision=lax.Precision.HIGHEST)
    part_real = factor_product(left_side[0], right_side[0]) - factor_product(left_side[1], right_side[1])
    part_imag = factor_product(left_side[0], right_side[1]) + factor_product(left_side[1], right_side[0])
    return jnp.stack([part_real, part_imag])

def response(filters, freq_bins):
    tap_index = jnp.arange(TAPS, dtype=jnp.int32)
    cosine_wave, sine_wave = wave_table(freq_bins, tap_index)
    filter_real = jnp.einsum('fk,wjk->fjw', cosine_wave, filters, precision=lax.Precision.HIGHEST)
    filter_imag = -jnp.einsum('fk,wjk->fjw', sine_wave, filters, precision=lax.Precision.HIGHEST)
    return (jnp.repeat(filter_real, RWIN, axis=2), jnp.repeat(filter_imag, RWIN, axis=2))

def apply_filter(extended, filter_real, filter_imag, source_count):
    sum_real = jnp.zeros(extended.shape[1:2] + (source_count,) + extended.shape[3:], jnp.float32)
    sum_imag = jnp.zeros_like(sum_real)
    for shifted in range(SPAN):
        part_real = extended[0, :, shifted:shifted + source_count, :]
        part_imag = extended[1, :, shifted:shifted + source_count, :]
        weight_real = filter_real[:, shifted][:, None, :]
        weight_imaginary = filter_imag[:, shifted][:, None, :]
        sum_real = sum_real + weight_real * part_real - weight_imaginary * part_imag
        sum_imag = sum_imag + weight_real * part_imag + weight_imaginary * part_real
    return jnp.stack([sum_real, sum_imag])

def reference(traces, filters):
    freq_bins = FLO + jnp.arange(NF, dtype=jnp.int32)
    cosine_wave, sine_wave = wave_table(freq_bins, jnp.arange(NT, dtype=jnp.int32))
    forward = (jnp.concatenate([cosine_wave, -sine_wave], 0) / jnp.float32(math.sqrt(NT))).astype(jnp.bfloat16)
    reciprocal_value = jnp.concatenate([cosine_wave, -sine_wave], 0).astype(jnp.bfloat16)
    flattened = traces.reshape(NS * NR, NT)
    spectra = jnp.dot(flattened, forward.T, preferred_element_type=jnp.float32).astype(jnp.bfloat16)
    spectrum = spectra.reshape(NS, NR, 2, NF).transpose(2, 3, 0, 1)
    widened = spectrum.astype(jnp.float32)
    order_one = (complex_product(widened, widened) / jnp.float32(math.sqrt(NS))).astype(jnp.bfloat16)
    order_two = complex_product(widened, order_one.astype(jnp.float32)) / jnp.float32(math.sqrt(NS))
    prediction = (order_one.astype(jnp.float32) - order_two).astype(jnp.bfloat16)
    rim_width = SPAN // 2
    extended = jnp.pad(prediction.astype(jnp.float32), ((0, 0), (0, 0), (rim_width, rim_width), (0, 0)))
    filter_real, filter_imag = response(filters, freq_bins)
    matched = apply_filter(extended, filter_real, filter_imag, NS).astype(jnp.bfloat16)
    matched_rows = matched.transpose(2, 3, 0, 1).reshape(NS * NR, 2 * NF)
    multiples = jnp.dot(matched_rows, reciprocal_value, preferred_element_type=jnp.float32) / jnp.float32(math.sqrt(NF))
    return (traces.astype(jnp.float32) - multiples.reshape(NS, NR, NT)).astype(jnp.bfloat16)
```

```python
import functools
import math

import jax
import jax.numpy as jnp
from jax import lax
from jax.experimental import pallas as pl
from jax.experimental.pallas import tpu as pltpu
from jax.sharding import PartitionSpec as P

NS = 640
NT = 1024
NF = 96
FLO = 8
TAPS = 64
SPAN = 7
RWIN = 40
LANES = 128
AXES = ("panel", "freq")


def wave_table(freq_bins, sample_index):
    phases = freq_bins[:, None] * sample_index[None, :] % NT
    angles = phases.astype(jnp.float32) * jnp.float32(2.0 * math.pi / NT)
    return (jnp.cos(angles), jnp.sin(angles))


def response(filters, freq_bins):
    tap_index = jnp.arange(TAPS, dtype=jnp.int32)
    cosine_wave, sine_wave = wave_table(freq_bins, tap_index)
    filter_real = jnp.einsum("fk,wjk->fjw", cosine_wave, filters, precision=lax.Precision.HIGHEST)
    filter_imag = -jnp.einsum("fk,wjk->fjw", sine_wave, filters, precision=lax.Precision.HIGHEST)
    return (jnp.repeat(filter_real, RWIN, axis=2), jnp.repeat(filter_imag, RWIN, axis=2))


class Plan:
    def __init__(self, shots, receivers, times, panels, columns):
        self.shots, self.receivers, self.times = shots, receivers, times
        self.panels, self.columns = panels, columns
        self.devices = panels * columns
        self.tail = receivers - LANES
        self.fits = (
            self.tail > 0
            and LANES % self.tail == 0
            and self.tail % 16 == 0
            and columns * self.tail == LANES
            and NF % self.devices == 0
        )
        if not self.fits:
            return
        self.fold = LANES // self.tail
        self.group = shots // self.fold
        self.fits = shots % 16 == 0 and shots % self.fold == 0 and self.group % 2 == 0
        self.slices = NF // self.devices
        self.rows = 2 * shots + 2 * self.group
        self.fits = self.fits and self.rows % 8 == 0
        self.side = NS
        self.runs = []
        for column in range(columns):
            self.runs.append((column * receivers, column * LANES, LANES))
        for column in range(columns):
            self.runs.append(
                (column * receivers + LANES, columns * LANES + column * self.tail, self.tail)
            )

    def cut(self, start, size):
        parts = []
        for natural, moved, length in self.runs:
            low, high = max(start, natural), min(start + size, natural + length)
            if low < high:
                parts.append((low - start, moved + low - natural, high - low))
        return parts


def spectrum_kernel(plan, step_size, table_ref, traces_ref, out_ref, wide_ref):
    step = pl.program_id(0)
    fold, group, shots, times = plan.fold, plan.group, plan.shots, plan.times

    def place(values, row, lane):
        for part in range(2):
            wide_ref[pl.ds(part * row[1] + row[0], NF, stride=plan.rows), :] = values[
                part * NF : (part + 1) * NF, lane * LANES : (lane + 1) * LANES
            ]

    contract = (((1,), (1,)), ((), ()))
    table = table_ref[...]
    for a in range(fold):
        main = traces_ref[a, :, :LANES, :].reshape(step_size * LANES, times)
        values = lax.dot_general(table, main, contract, preferred_element_type=jnp.float32)
        for j in range(step_size):
            place(values, (a * group + step * step_size + j, shots), j)
    tails = jnp.concatenate(
        [
            traces_ref[:, j, LANES:, :].reshape(fold * plan.tail, times)
            for j in range(step_size)
        ],
        axis=0,
    )
    values = lax.dot_general(table, tails, contract, preferred_element_type=jnp.float32)
    for j in range(step_size):
        place(values, (2 * shots + step * step_size + j, group), j)

    @pl.when(step == pl.num_programs(0) - 1)
    def _():
        @pl.loop(0, NF)
        def _(f):
            rows = pl.ds(pl.multiple_of(f * plan.rows, 8), plan.rows)
            out_ref[rows, :] = wide_ref[rows, :].astype(jnp.bfloat16)


def spectrum(plan, traces, table):
    fold, group = plan.fold, plan.group
    step_size = 2
    shape = (NF * plan.rows, LANES)
    return pl.pallas_call(
        functools.partial(spectrum_kernel, plan, step_size),
        grid=(group // step_size,),
        out_shape=jax.ShapeDtypeStruct(shape, jnp.bfloat16),
        in_specs=[
            pl.BlockSpec(table.shape, lambda i: (0, 0)),
            pl.BlockSpec((fold, step_size, plan.receivers, plan.times), lambda i: (0, i, 0, 0)),
        ],
        out_specs=pl.BlockSpec(shape, lambda i: (0, 0)),
        scratch_shapes=[pltpu.VMEM(shape, jnp.float32)],
        name="spectrum",
    )(table, traces.reshape(fold, group, plan.receivers, plan.times))


def inverse_kernel(plan, step_size, table_ref, matched_ref, traces_ref, out_ref, wide_ref):
    step = pl.program_id(0)
    fold, group, shots, times = plan.fold, plan.group, plan.shots, plan.times
    scale = jnp.float32(1.0 / math.sqrt(NF))

    @pl.when(step == 0)
    def _():
        @pl.loop(0, NF)
        def _(f):
            rows = pl.ds(pl.multiple_of(f * plan.rows, 8), plan.rows)
            wide_ref[rows, :] = matched_ref[rows, :].astype(jnp.float32)

    def fetch(row, spread):
        parts = [
            wide_ref[pl.ds(part * spread + row, NF, stride=plan.rows), :].T for part in range(2)
        ]
        return jnp.concatenate(parts, axis=1).astype(jnp.bfloat16)

    table = table_ref[...]
    for j in range(step_size):
        for a in range(fold):
            values = jnp.dot(
                fetch(a * group + step * step_size + j, shots),
                table,
                preferred_element_type=jnp.float32,
            )
            own = traces_ref[a, j, :LANES, :].astype(jnp.float32)
            out_ref[a, j, :LANES, :] = (own - values * scale).astype(jnp.bfloat16)
        values = jnp.dot(
            fetch(2 * shots + step * step_size + j, group),
            table,
            preferred_element_type=jnp.float32,
        )
        own = traces_ref[:, j, LANES:, :].astype(jnp.float32)
        values = values.reshape(fold, plan.tail, times)
        out_ref[:, j, LANES:, :] = (own - values * scale).astype(jnp.bfloat16)


def subtract(plan, traces, matched, table):
    fold, group = plan.fold, plan.group
    step_size = 2
    shape = (NF * plan.rows, LANES)
    block = pl.BlockSpec((fold, step_size, plan.receivers, plan.times), lambda i: (0, i, 0, 0))
    view = (fold, group, plan.receivers, plan.times)
    out = pl.pallas_call(
        functools.partial(inverse_kernel, plan, step_size),
        grid=(group // step_size,),
        out_shape=jax.ShapeDtypeStruct(view, jnp.bfloat16),
        in_specs=[
            pl.BlockSpec(table.shape, lambda i: (0, 0)),
            pl.BlockSpec(shape, lambda i: (0, 0)),
            block,
        ],
        out_specs=block,
        scratch_shapes=[pltpu.VMEM(shape, jnp.float32)],
        name="inverse",
    )(table, matched, traces.reshape(view))
    return out.reshape(traces.shape)


RIM = 8
CHUNK = 256


def predict_kernel(
    plan, weight_ref, in_ref, out_ref, left_ref, right_ref, first_ref, side_ref, ahead_ref, fold_ref
):
    shots, group, fold, tail = plan.shots, plan.group, plan.fold, plan.tail
    side, columns, panels = plan.side, plan.columns, plan.panels
    scale = jnp.float32(1.0 / math.sqrt(NS))
    tails_at = columns * LANES

    for panel in range(panels):
        parts = plan.cut(panel * shots, shots)
        for column in range(columns):
            source = panel * columns + column
            for part in range(2):
                lanes = slice(part * side + column * LANES, part * side + (column + 1) * LANES)
                for offset, row, length in parts:
                    at = part * shots + offset
                    left_ref[row : row + length, lanes] = in_ref[source, at : at + length, :]
            packed = in_ref[source, 2 * shots :, :].astype(jnp.float32)
            for part in range(2):
                for a in range(fold):
                    side_ref[
                        part,
                        panel * shots + a * group : panel * shots + (a + 1) * group,
                        column * tail : (column + 1) * tail,
                    ] = packed[part * group : (part + 1) * group, a * tail : (a + 1) * tail]
    for natural, moved, length in plan.runs:
        for part in range(2):
            left_ref[
                moved : moved + length, part * side + tails_at : (part + 1) * side
            ] = side_ref[part, natural : natural + length, :].astype(jnp.bfloat16)

    def fill(from_ref):
        right_ref[:side, :] = from_ref[...]
        right_ref[side:, :side] = -from_ref[:, side:]
        right_ref[side:, side:] = from_ref[:, :side]

    fill(left_ref)

    @pl.loop(0, 2 * side // CHUNK)
    def _(k):
        lanes = pl.ds(pl.multiple_of(k * CHUNK, CHUNK), CHUNK)
        total = jnp.dot(left_ref[...], right_ref[:, lanes], preferred_element_type=jnp.float32)
        first_ref[:, lanes] = (total * scale).astype(jnp.bfloat16)

    fill(first_ref)
    ahead_ref[:RIM, :] = jnp.zeros((RIM, 2 * side), jnp.float32)
    ahead_ref[RIM + side :, :] = jnp.zeros((RIM, 2 * side), jnp.float32)

    @pl.loop(0, 2 * side // CHUNK)
    def _(k):
        lanes = pl.ds(pl.multiple_of(k * CHUNK, CHUNK), CHUNK)
        total = jnp.dot(left_ref[...], right_ref[:, lanes], preferred_element_type=jnp.float32)
        value = first_ref[:, lanes].astype(jnp.float32) - total * scale
        value = value.astype(jnp.bfloat16).astype(jnp.float32)
        for natural, moved, length in plan.runs:
            ahead_ref[RIM + natural : RIM + natural + length, lanes] = value[moved : moved + length]

    @pl.loop(0, panels)
    def _(panel):
        rows = pl.ds(pl.multiple_of(panel * shots, 8), shots + 2 * RIM)
        for column in range(columns + 1):
            at = column * LANES
            real = ahead_ref[rows, at : at + LANES]
            imag = ahead_ref[rows, side + at : side + at + LANES]
            sum_real = sum_imag = None
            for j in range(SPAN):
                low = RIM - SPAN // 2 + j
                part_real, part_imag = real[low : low + shots], imag[low : low + shots]
                weight_real = weight_ref[0, j : j + 1, at : at + LANES]
                weight_imag = weight_ref[1, j : j + 1, at : at + LANES]
                term_real = weight_real * part_real - weight_imag * part_imag
                term_imag = weight_real * part_imag + weight_imag * part_real
                sum_real = term_real if j == 0 else sum_real + term_real
                sum_imag = term_imag if j == 0 else sum_imag + term_imag
            if column < columns:
                target = panel * columns + column
                out_ref[target, :shots, :] = sum_real.astype(jnp.bfloat16)
                out_ref[target, shots : 2 * shots, :] = sum_imag.astype(jnp.bfloat16)
                continue
            for part, total in enumerate((sum_real, sum_imag)):
                for other in range(columns):
                    for a in range(fold):
                        fold_ref[
                            other,
                            part * group : (part + 1) * group,
                            a * tail : (a + 1) * tail,
                        ] = total[a * group : (a + 1) * group, other * tail : (other + 1) * tail]
            for other in range(columns):
                out_ref[panel * columns + other, 2 * shots :, :] = fold_ref[other].astype(
                    jnp.bfloat16
                )


def predict(plan, blocks, weights):
    side = plan.side
    block = pl.BlockSpec((plan.devices, plan.rows, LANES), lambda f: (0, f, 0))
    return pl.pallas_call(
        functools.partial(predict_kernel, plan),
        grid=(plan.slices,),
        out_shape=jax.ShapeDtypeStruct(blocks.shape, jnp.bfloat16),
        in_specs=[pl.BlockSpec((None, 2, 8, side), lambda f: (f, 0, 0, 0)), block],
        out_specs=block,
        scratch_shapes=[
            pltpu.VMEM((side, 2 * side), jnp.bfloat16),
            pltpu.VMEM((2 * side, 2 * side), jnp.bfloat16),
            pltpu.VMEM((side, 2 * side), jnp.bfloat16),
            pltpu.VMEM((2, side, LANES), jnp.float32),
            pltpu.VMEM((side + 2 * RIM, 2 * side), jnp.float32),
            pltpu.VMEM((plan.columns, 2 * plan.group, LANES), jnp.float32),
        ],
        name="predict",
    )(weights, blocks)


def moved_lanes(plan, values):
    split = values.reshape(values.shape[:-1] + (plan.columns, plan.receivers))
    main = split[..., :LANES].reshape(values.shape[:-1] + (plan.columns * LANES,))
    tail = split[..., LANES:].reshape(values.shape[:-1] + (plan.columns * plan.tail,))
    return jnp.concatenate([main, tail], axis=-1)


def per_device(plan, traces, filters):
    freq_bins = FLO + jnp.arange(NF, dtype=jnp.int32)
    cosine_wave, sine_wave = wave_table(freq_bins, jnp.arange(NT, dtype=jnp.int32))
    waves = jnp.concatenate([cosine_wave, -sine_wave], 0)
    forward = (waves / jnp.float32(math.sqrt(NT))).astype(jnp.bfloat16)
    inverse = waves.astype(jnp.bfloat16)
    wire = (plan.devices, plan.slices * plan.rows, LANES)

    spectra = spectrum(plan, traces, forward).reshape(wire)
    received = lax.all_to_all(spectra, AXES, split_axis=0, concat_axis=0, tiled=True)
    own = lax.axis_index(AXES) * plan.slices + jnp.arange(plan.slices, dtype=jnp.int32)
    weights = jnp.stack([moved_lanes(plan, w) for w in response(filters, FLO + own)], axis=1)
    weights = jnp.pad(weights, ((0, 0), (0, 0), (0, 8 - SPAN), (0, 0)))
    matched = predict(plan, received, weights)
    returned = lax.all_to_all(matched, AXES, split_axis=0, concat_axis=0, tiled=True)
    return subtract(plan, traces, returned.reshape(NF * plan.rows, LANES), inverse)


def complex_product(left_side, right_side):
    product = functools.partial(
        jnp.einsum, "gjo,god->gjd", preferred_element_type=jnp.float32
    )
    part_real = product(left_side[0], right_side[0]) - product(left_side[1], right_side[1])
    part_imag = product(left_side[0], right_side[1]) + product(left_side[1], right_side[0])
    return jnp.stack([part_real, part_imag])


def apply_filter(extended, filter_real, filter_imag, source_count):
    sum_real = jnp.zeros(extended.shape[1:2] + (source_count,) + extended.shape[3:], jnp.float32)
    sum_imag = jnp.zeros_like(sum_real)
    for shifted in range(SPAN):
        part_real = extended[0, :, shifted : shifted + source_count, :]
        part_imag = extended[1, :, shifted : shifted + source_count, :]
        weight_real = filter_real[:, shifted][:, None, :]
        weight_imaginary = filter_imag[:, shifted][:, None, :]
        sum_real = sum_real + weight_real * part_real - weight_imaginary * part_imag
        sum_imag = sum_imag + weight_real * part_imag + weight_imaginary * part_real
    return jnp.stack([sum_real, sum_imag])


def per_device_general(traces, filters):
    shot_rows, receiver_cols, time_sample_count = traces.shape
    rim_width = SPAN // 2
    scale_sources = jnp.float32(math.sqrt(NS))
    freq_bins = FLO + jnp.arange(NF, dtype=jnp.int32)
    cosine_wave, sine_wave = wave_table(freq_bins, jnp.arange(NT, dtype=jnp.int32))
    waves = jnp.concatenate([cosine_wave, -sine_wave], 0)
    forward = (waves / jnp.float32(math.sqrt(NT))).astype(jnp.bfloat16)
    spectra = jnp.einsum("srt,ct->csr", traces, forward, preferred_element_type=jnp.float32)
    spectra = spectra.astype(jnp.bfloat16).reshape(2, NF, shot_rows, receiver_cols)
    columns = lax.all_to_all(spectra, "panel", split_axis=1, concat_axis=2, tiled=True)
    slice_count = columns.shape[1]
    first_slice = lax.axis_index("panel") * slice_count
    complete = lax.all_gather(columns, "freq", axis=3, tiled=True)
    order_one = (complex_product(complete, columns) / scale_sources).astype(jnp.bfloat16)
    order_two = complex_product(complete, order_one) / scale_sources
    prediction = (order_one.astype(jnp.float32) - order_two).astype(jnp.bfloat16)
    extended = jnp.pad(
        prediction.astype(jnp.float32), ((0, 0), (0, 0), (rim_width, rim_width), (0, 0))
    )
    own_bins = FLO + first_slice + jnp.arange(slice_count, dtype=jnp.int32)
    filter_real, filter_imag = response(filters, own_bins)
    receiver_start = lax.axis_index("freq") * receiver_cols
    filter_real = lax.dynamic_slice_in_dim(filter_real, receiver_start, receiver_cols, 2)
    filter_imag = lax.dynamic_slice_in_dim(filter_imag, receiver_start, receiver_cols, 2)
    matched = apply_filter(extended, filter_real, filter_imag, NS)
    returned = lax.all_to_all(
        matched.astype(jnp.bfloat16), "panel", split_axis=2, concat_axis=1, tiled=True
    )
    matched_rows = returned.reshape(2 * NF, shot_rows, receiver_cols)
    multiples = jnp.einsum(
        "csr,ct->srt", matched_rows, waves.astype(jnp.bfloat16), preferred_element_type=jnp.float32
    )
    multiples = multiples / jnp.float32(math.sqrt(NF))
    return (traces.astype(jnp.float32) - multiples).astype(jnp.bfloat16)


def solution(mesh):
    placed = (P("panel", "freq", None), P())
    panels, columns = mesh.shape["panel"], mesh.shape["freq"]

    def body(traces, filters):
        shots, receivers, times = traces.shape
        plan = Plan(shots, receivers, times, panels, columns)
        if plan.fits:
            return per_device(plan, traces, filters)
        return per_device_general(traces, filters)

    return jax.shard_map(
        body, mesh=mesh, in_specs=placed, out_specs=P("panel", "freq", None), check_vma=False
    )
```

```python
import functools
import math

import jax
import jax.numpy as jnp
from jax import lax
from jax.experimental import pallas as pl
from jax.experimental.pallas import tpu as pltpu
from jax.sharding import PartitionSpec as P

NS = 640
NT = 1024
NF = 96
FLO = 8
TAPS = 64
SPAN = 7
RWIN = 40
LANES = 128
AXES = ("panel", "freq")
MESH = pl.DeviceIdType.MESH


def wave_table(freq_bins, sample_index):
    phases = freq_bins[:, None] * sample_index[None, :] % NT
    angles = phases.astype(jnp.float32) * jnp.float32(2.0 * math.pi / NT)
    return (jnp.cos(angles), jnp.sin(angles))


def response(filters, freq_bins):
    tap_index = jnp.arange(TAPS, dtype=jnp.int32)
    cosine_wave, sine_wave = wave_table(freq_bins, tap_index)
    filter_real = jnp.einsum("fk,wjk->fjw", cosine_wave, filters, precision=lax.Precision.HIGHEST)
    filter_imag = -jnp.einsum("fk,wjk->fjw", sine_wave, filters, precision=lax.Precision.HIGHEST)
    return (jnp.repeat(filter_real, RWIN, axis=2), jnp.repeat(filter_imag, RWIN, axis=2))


class Plan:
    def __init__(self, shots, receivers, times, panels, columns):
        self.shots, self.receivers, self.times = shots, receivers, times
        self.panels, self.columns = panels, columns
        self.devices = panels * columns
        self.tail = receivers - LANES
        self.fits = (
            self.tail > 0
            and LANES % self.tail == 0
            and self.tail % 16 == 0
            and columns * self.tail == LANES
            and NF % self.devices == 0
        )
        if not self.fits:
            return
        self.fold = LANES // self.tail
        self.group = shots // self.fold
        self.fits = shots % 16 == 0 and shots % self.fold == 0 and self.group % 2 == 0
        self.slices = NF // self.devices
        self.rows = 2 * shots + 2 * self.group
        self.fits = self.fits and self.rows % 8 == 0
        self.side = NS
        self.runs = []
        for column in range(columns):
            self.runs.append((column * receivers, column * LANES, LANES))
        for column in range(columns):
            self.runs.append(
                (column * receivers + LANES, columns * LANES + column * self.tail, self.tail)
            )

    def cut(self, start, size):
        parts = []
        for natural, moved, length in self.runs:
            low, high = max(start, natural), min(start + size, natural + length)
            if low < high:
                parts.append((low - start, moved + low - natural, high - low))
        return parts


def spectrum_kernel(plan, step_size, table_ref, traces_ref, out_ref, wide_ref):
    step = pl.program_id(0)
    fold, group, shots, times = plan.fold, plan.group, plan.shots, plan.times

    def place(values, row, lane):
        for part in range(2):
            wide_ref[pl.ds(part * row[1] + row[0], NF, stride=plan.rows), :] = values[
                part * NF : (part + 1) * NF, lane * LANES : (lane + 1) * LANES
            ]

    contract = (((1,), (1,)), ((), ()))
    table = table_ref[...]
    for a in range(fold):
        main = traces_ref[a, :, :LANES, :].reshape(step_size * LANES, times)
        values = lax.dot_general(table, main, contract, preferred_element_type=jnp.float32)
        for j in range(step_size):
            place(values, (a * group + step * step_size + j, shots), j)
    tails = jnp.concatenate(
        [
            traces_ref[:, j, LANES:, :].reshape(fold * plan.tail, times)
            for j in range(step_size)
        ],
        axis=0,
    )
    values = lax.dot_general(table, tails, contract, preferred_element_type=jnp.float32)
    for j in range(step_size):
        place(values, (2 * shots + step * step_size + j, group), j)

    @pl.when(step == pl.num_programs(0) - 1)
    def _():
        @pl.loop(0, NF)
        def _(f):
            rows = pl.ds(pl.multiple_of(f * plan.rows, 8), plan.rows)
            out_ref[rows, :] = wide_ref[rows, :].astype(jnp.bfloat16)


def spectrum(plan, traces, table):
    fold, group = plan.fold, plan.group
    step_size = 2
    shape = (NF * plan.rows, LANES)
    return pl.pallas_call(
        functools.partial(spectrum_kernel, plan, step_size),
        grid=(group // step_size,),
        out_shape=jax.ShapeDtypeStruct(shape, jnp.bfloat16),
        in_specs=[
            pl.BlockSpec(table.shape, lambda i: (0, 0)),
            pl.BlockSpec((fold, step_size, plan.receivers, plan.times), lambda i: (0, i, 0, 0)),
        ],
        out_specs=pl.BlockSpec(shape, lambda i: (0, 0)),
        scratch_shapes=[pltpu.VMEM(shape, jnp.float32)],
        name="spectrum",
    )(table, traces.reshape(fold, group, plan.receivers, plan.times))


def inverse_kernel(plan, step_size, table_ref, matched_ref, traces_ref, out_ref, wide_ref):
    step = pl.program_id(0)
    fold, group, shots, times = plan.fold, plan.group, plan.shots, plan.times
    scale = jnp.float32(1.0 / math.sqrt(NF))

    @pl.when(step == 0)
    def _():
        @pl.loop(0, NF)
        def _(f):
            rows = pl.ds(pl.multiple_of(f * plan.rows, 8), plan.rows)
            wide_ref[rows, :] = matched_ref[rows, :].astype(jnp.float32)

    def fetch(row, spread):
        parts = [
            wide_ref[pl.ds(part * spread + row, NF, stride=plan.rows), :].T for part in range(2)
        ]
        return jnp.concatenate(parts, axis=1).astype(jnp.bfloat16)

    table = table_ref[...]
    for j in range(step_size):
        for a in range(fold):
            values = jnp.dot(
                fetch(a * group + step * step_size + j, shots),
                table,
                preferred_element_type=jnp.float32,
            )
            own = traces_ref[a, j, :LANES, :].astype(jnp.float32)
            out_ref[a, j, :LANES, :] = (own - values * scale).astype(jnp.bfloat16)
        values = jnp.dot(
            fetch(2 * shots + step * step_size + j, group),
            table,
            preferred_element_type=jnp.float32,
        )
        own = traces_ref[:, j, LANES:, :].astype(jnp.float32)
        values = values.reshape(fold, plan.tail, times)
        out_ref[:, j, LANES:, :] = (own - values * scale).astype(jnp.bfloat16)


def subtract(plan, traces, matched, table):
    fold, group = plan.fold, plan.group
    step_size = 2
    shape = (NF * plan.rows, LANES)
    block = pl.BlockSpec((fold, step_size, plan.receivers, plan.times), lambda i: (0, i, 0, 0))
    view = (fold, group, plan.receivers, plan.times)
    out = pl.pallas_call(
        functools.partial(inverse_kernel, plan, step_size),
        grid=(group // step_size,),
        out_shape=jax.ShapeDtypeStruct(view, jnp.bfloat16),
        in_specs=[
            pl.BlockSpec(table.shape, lambda i: (0, 0)),
            pl.BlockSpec(shape, lambda i: (0, 0)),
            block,
        ],
        out_specs=block,
        scratch_shapes=[pltpu.VMEM(shape, jnp.float32)],
        name="inverse",
    )(table, matched, traces.reshape(view))
    return out.reshape(traces.shape)


RIM = 8
CHUNK = 256


def predict_kernel(
    plan,
    weight_ref,
    sent_ref,
    back_ref,
    got_ref,
    out_ref,
    left_ref,
    right_ref,
    first_ref,
    side_ref,
    ahead_ref,
    fold_ref,
    send_sem,
    got_sem,
    own_sem,
    back_send_sem,
    back_sem,
    back_own_sem,
):
    shots, group, fold, tail = plan.shots, plan.group, plan.fold, plan.tail
    side, columns, panels, devices = plan.side, plan.columns, plan.panels, plan.devices
    rows_of, slices = plan.rows, plan.slices
    scale = jnp.float32(1.0 / math.sqrt(NS))
    tails_at = columns * LANES
    my_panel, my_column = lax.axis_index("panel"), lax.axis_index("freq")
    me = my_panel * columns + my_column

    def place_of(device):
        return {"panel": device // columns, "freq": lax.rem(device, columns)}

    def partner(i):
        shift = devices // 2 + (1 - 2 * lax.rem(i, 2)) * ((i + 1) // 2)
        return lax.rem(me + shift, devices)

    barrier = pltpu.get_barrier_semaphore()

    @pl.loop(0, devices - 1)
    def _(i):
        pl.semaphore_signal(barrier, inc=1, device_id=place_of(partner(i)), device_id_type=MESH)

    pl.semaphore_wait(barrier, devices - 1)

    def rows_at(f):
        return pl.ds(pl.multiple_of(f * rows_of, 8), rows_of)

    @pl.loop(0, slices)
    def _(f):
        pltpu.make_async_copy(
            sent_ref.at[me, rows_at(f)], got_ref.at[f, me], own_sem.at[f]
        ).start()

        @pl.loop(0, devices - 1)
        def _(i):
            device = partner(i)
            pltpu.make_async_remote_copy(
                src_ref=sent_ref.at[device, rows_at(f)],
                dst_ref=got_ref.at[f, me],
                send_sem=send_sem,
                recv_sem=got_sem.at[f],
                device_id=place_of(device),
                device_id_type=MESH,
            ).start()

    ahead_ref[:RIM, :] = jnp.zeros((RIM, 2 * side), jnp.float32)
    ahead_ref[RIM + side :, :] = jnp.zeros((RIM, 2 * side), jnp.float32)

    def fill(from_ref):
        right_ref[:side, :] = from_ref[...]
        right_ref[side:, :side] = -from_ref[:, side:]
        right_ref[side:, side:] = from_ref[:, :side]

    def panel_at(i):
        return lax.rem(my_panel + panels // 2 + i, panels)

    def send_back(f, panel):
        for column in range(columns):
            device = panel * columns + column
            own = device == me

            @pl.when(own)
            def _():
                pltpu.make_async_copy(
                    out_ref.at[f, device], back_ref.at[me, rows_at(f)], back_own_sem.at[f]
                ).start()

            @pl.when(jnp.logical_not(own))
            def _():
                pltpu.make_async_remote_copy(
                    src_ref=out_ref.at[f, device],
                    dst_ref=back_ref.at[me, rows_at(f)],
                    send_sem=back_send_sem,
                    recv_sem=back_sem,
                    device_id={"panel": panel, "freq": column},
                    device_id_type=MESH,
                ).start()

    @pl.loop(0, slices)
    def _(f):
        pltpu.make_async_copy(
            sent_ref.at[me, rows_at(f)], got_ref.at[f, me], own_sem.at[f]
        ).wait()
        others = got_ref.at[f, pl.ds(0, devices - 1)]
        pltpu.make_async_copy(others, others, got_sem.at[f]).wait()

        for panel in range(panels):
            parts = plan.cut(panel * shots, shots)
            for column in range(columns):
                source = panel * columns + column
                for part in range(2):
                    lanes = slice(
                        part * side + column * LANES, part * side + (column + 1) * LANES
                    )
                    for offset, row, length in parts:
                        at = part * shots + offset
                        left_ref[row : row + length, lanes] = got_ref[
                            f, source, at : at + length, :
                        ]
                packed = got_ref[f, source, 2 * shots :, :].astype(jnp.float32)
                for part in range(2):
                    for a in range(fold):
                        side_ref[
                            part,
                            panel * shots + a * group : panel * shots + (a + 1) * group,
                            column * tail : (column + 1) * tail,
                        ] = packed[part * group : (part + 1) * group, a * tail : (a + 1) * tail]
        for natural, moved, length in plan.runs:
            for part in range(2):
                left_ref[
                    moved : moved + length, part * side + tails_at : (part + 1) * side
                ] = side_ref[part, natural : natural + length, :].astype(jnp.bfloat16)

        fill(left_ref)

        @pl.loop(0, 2 * side // CHUNK)
        def _(k):
            lanes = pl.ds(pl.multiple_of(k * CHUNK, CHUNK), CHUNK)
            total = jnp.dot(left_ref[...], right_ref[:, lanes], preferred_element_type=jnp.float32)
            first_ref[:, lanes] = (total * scale).astype(jnp.bfloat16)

        fill(first_ref)

        @pl.loop(0, 2 * side // CHUNK)
        def _(k):
            lanes = pl.ds(pl.multiple_of(k * CHUNK, CHUNK), CHUNK)
            total = jnp.dot(left_ref[...], right_ref[:, lanes], preferred_element_type=jnp.float32)
            value = first_ref[:, lanes].astype(jnp.float32) - total * scale
            value = value.astype(jnp.bfloat16).astype(jnp.float32)
            for natural, moved, length in plan.runs:
                ahead_ref[RIM + natural : RIM + natural + length, lanes] = value[
                    moved : moved + length
                ]

        @pl.loop(0, panels)
        def _(i):
            panel = panel_at(i)
            rows = pl.ds(pl.multiple_of(panel * shots, 8), shots + 2 * RIM)
            for column in range(columns + 1):
                at = column * LANES
                real = ahead_ref[rows, at : at + LANES]
                imag = ahead_ref[rows, side + at : side + at + LANES]
                sum_real = sum_imag = None
                for j in range(SPAN):
                    low = RIM - SPAN // 2 + j
                    part_real, part_imag = real[low : low + shots], imag[low : low + shots]
                    weight_real = weight_ref[f, 0, j : j + 1, at : at + LANES]
                    weight_imag = weight_ref[f, 1, j : j + 1, at : at + LANES]
                    term_real = weight_real * part_real - weight_imag * part_imag
                    term_imag = weight_real * part_imag + weight_imag * part_real
                    sum_real = term_real if j == 0 else sum_real + term_real
                    sum_imag = term_imag if j == 0 else sum_imag + term_imag
                if column < columns:
                    target = panel * columns + column
                    out_ref[f, target, :shots, :] = sum_real.astype(jnp.bfloat16)
                    out_ref[f, target, shots : 2 * shots, :] = sum_imag.astype(jnp.bfloat16)
                    continue
                for part, total in enumerate((sum_real, sum_imag)):
                    for other in range(columns):
                        for a in range(fold):
                            fold_ref[
                                other,
                                part * group : (part + 1) * group,
                                a * tail : (a + 1) * tail,
                            ] = total[
                                a * group : (a + 1) * group, other * tail : (other + 1) * tail
                            ]
                for other in range(columns):
                    out_ref[f, panel * columns + other, 2 * shots :, :] = fold_ref[other].astype(
                        jnp.bfloat16
                    )

            @pl.when(i > 0)
            def _():
                send_back(f, panel_at(i - 1))

        send_back(f, panel_at(panels - 1))

    others = sent_ref.at[pl.ds(0, devices - 1)]
    pltpu.make_async_copy(others, others, send_sem).wait()

    @pl.loop(0, slices)
    def _(f):
        pltpu.make_async_copy(
            out_ref.at[f, me], back_ref.at[me, rows_at(f)], back_own_sem.at[f]
        ).wait()

    others = back_ref.at[pl.ds(0, devices - 1)]
    pltpu.make_async_copy(others, others, back_send_sem).wait()
    pltpu.make_async_copy(others, others, back_sem).wait()


def predict(plan, blocks, weights):
    side = plan.side
    held = (plan.slices, plan.devices, plan.rows, LANES)
    return pl.pallas_call(
        functools.partial(predict_kernel, plan),
        out_shape=jax.ShapeDtypeStruct(blocks.shape, jnp.bfloat16),
        in_specs=[pl.BlockSpec(memory_space=pltpu.VMEM), pl.BlockSpec(memory_space=pl.ANY)],
        out_specs=pl.BlockSpec(memory_space=pl.ANY),
        scratch_shapes=[
            pltpu.VMEM(held, jnp.bfloat16),
            pltpu.VMEM(held, jnp.bfloat16),
            pltpu.VMEM((side, 2 * side), jnp.bfloat16),
            pltpu.VMEM((2 * side, 2 * side), jnp.bfloat16),
            pltpu.VMEM((side, 2 * side), jnp.bfloat16),
            pltpu.VMEM((2, side, LANES), jnp.float32),
            pltpu.VMEM((side + 2 * RIM, 2 * side), jnp.float32),
            pltpu.VMEM((plan.columns, 2 * plan.group, LANES), jnp.float32),
            pltpu.SemaphoreType.DMA,
            pltpu.SemaphoreType.DMA((plan.slices,)),
            pltpu.SemaphoreType.DMA((plan.slices,)),
            pltpu.SemaphoreType.DMA,
            pltpu.SemaphoreType.DMA,
            pltpu.SemaphoreType.DMA((plan.slices,)),
        ],
        compiler_params=pltpu.CompilerParams(collective_id=0, has_side_effects=True),
        name="predict",
    )(weights, blocks)


def moved_lanes(plan, values):
    split = values.reshape(values.shape[:-1] + (plan.columns, plan.receivers))
    main = split[..., :LANES].reshape(values.shape[:-1] + (plan.columns * LANES,))
    tail = split[..., LANES:].reshape(values.shape[:-1] + (plan.columns * plan.tail,))
    return jnp.concatenate([main, tail], axis=-1)


def per_device(plan, traces, filters):
    freq_bins = FLO + jnp.arange(NF, dtype=jnp.int32)
    cosine_wave, sine_wave = wave_table(freq_bins, jnp.arange(NT, dtype=jnp.int32))
    waves = jnp.concatenate([cosine_wave, -sine_wave], 0)
    forward = (waves / jnp.float32(math.sqrt(NT))).astype(jnp.bfloat16)
    inverse = waves.astype(jnp.bfloat16)
    wire = (plan.devices, plan.slices * plan.rows, LANES)

    spectra = spectrum(plan, traces, forward).reshape(wire)
    own = lax.axis_index(AXES) * plan.slices + jnp.arange(plan.slices, dtype=jnp.int32)
    weights = jnp.stack([moved_lanes(plan, w) for w in response(filters, FLO + own)], axis=1)
    weights = jnp.pad(weights, ((0, 0), (0, 0), (0, 8 - SPAN), (0, 0)))
    returned = predict(plan, spectra, weights)
    return subtract(plan, traces, returned.reshape(NF * plan.rows, LANES), inverse)


def complex_product(left_side, right_side):
    product = functools.partial(
        jnp.einsum, "gjo,god->gjd", preferred_element_type=jnp.float32
    )
    part_real = product(left_side[0], right_side[0]) - product(left_side[1], right_side[1])
    part_imag = product(left_side[0], right_side[1]) + product(left_side[1], right_side[0])
    return jnp.stack([part_real, part_imag])


def apply_filter(extended, filter_real, filter_imag, source_count):
    sum_real = jnp.zeros(extended.shape[1:2] + (source_count,) + extended.shape[3:], jnp.float32)
    sum_imag = jnp.zeros_like(sum_real)
    for shifted in range(SPAN):
        part_real = extended[0, :, shifted : shifted + source_count, :]
        part_imag = extended[1, :, shifted : shifted + source_count, :]
        weight_real = filter_real[:, shifted][:, None, :]
        weight_imaginary = filter_imag[:, shifted][:, None, :]
        sum_real = sum_real + weight_real * part_real - weight_imaginary * part_imag
        sum_imag = sum_imag + weight_real * part_imag + weight_imaginary * part_real
    return jnp.stack([sum_real, sum_imag])


def per_device_general(traces, filters):
    shot_rows, receiver_cols, time_sample_count = traces.shape
    rim_width = SPAN // 2
    scale_sources = jnp.float32(math.sqrt(NS))
    freq_bins = FLO + jnp.arange(NF, dtype=jnp.int32)
    cosine_wave, sine_wave = wave_table(freq_bins, jnp.arange(NT, dtype=jnp.int32))
    waves = jnp.concatenate([cosine_wave, -sine_wave], 0)
    forward = (waves / jnp.float32(math.sqrt(NT))).astype(jnp.bfloat16)
    spectra = jnp.einsum("srt,ct->csr", traces, forward, preferred_element_type=jnp.float32)
    spectra = spectra.astype(jnp.bfloat16).reshape(2, NF, shot_rows, receiver_cols)
    columns = lax.all_to_all(spectra, "panel", split_axis=1, concat_axis=2, tiled=True)
    slice_count = columns.shape[1]
    first_slice = lax.axis_index("panel") * slice_count
    complete = lax.all_gather(columns, "freq", axis=3, tiled=True)
    order_one = (complex_product(complete, columns) / scale_sources).astype(jnp.bfloat16)
    order_two = complex_product(complete, order_one) / scale_sources
    prediction = (order_one.astype(jnp.float32) - order_two).astype(jnp.bfloat16)
    extended = jnp.pad(
        prediction.astype(jnp.float32), ((0, 0), (0, 0), (rim_width, rim_width), (0, 0))
    )
    own_bins = FLO + first_slice + jnp.arange(slice_count, dtype=jnp.int32)
    filter_real, filter_imag = response(filters, own_bins)
    receiver_start = lax.axis_index("freq") * receiver_cols
    filter_real = lax.dynamic_slice_in_dim(filter_real, receiver_start, receiver_cols, 2)
    filter_imag = lax.dynamic_slice_in_dim(filter_imag, receiver_start, receiver_cols, 2)
    matched = apply_filter(extended, filter_real, filter_imag, NS)
    returned = lax.all_to_all(
        matched.astype(jnp.bfloat16), "panel", split_axis=2, concat_axis=1, tiled=True
    )
    matched_rows = returned.reshape(2 * NF, shot_rows, receiver_cols)
    multiples = jnp.einsum(
        "csr,ct->srt", matched_rows, waves.astype(jnp.bfloat16), preferred_element_type=jnp.float32
    )
    multiples = multiples / jnp.float32(math.sqrt(NF))
    return (traces.astype(jnp.float32) - multiples).astype(jnp.bfloat16)


def solution(mesh):
    placed = (P("panel", "freq", None), P())
    panels, columns = mesh.shape["panel"], mesh.shape["freq"]

    def body(traces, filters):
        shots, receivers, times = traces.shape
        plan = Plan(shots, receivers, times, panels, columns)
        if plan.fits:
            return per_device(plan, traces, filters)
        return per_device_general(traces, filters)

    return jax.shard_map(
        body, mesh=mesh, in_specs=placed, out_specs=P("panel", "freq", None), check_vma=False
    )
```
